32 devices in a mesh: ctx: 8 (over y, x, core), ch: 4 (over z).
Axes of the slice: x: 2, y: 2, z: 4, core: 2. Of those that a mesh axis runs over, the one named last changes fastest.
Arguments:
- q_short: bfloat16 [1024, 8192], P('ctx', 'ch'), may hold values from -6 to 6
- k_short: bfloat16 [1024, 8192], P('ctx', 'ch'), may hold values from -6 to 6
- v_input: bfloat16 [1024, 8192], P('ctx', 'ch'), may hold values from -6 to 6
- q_long: bfloat16 [1024, 8192], P('ctx', 'ch'), may hold values from -6 to 6
- k_long: bfloat16 [1024, 8192], P('ctx', 'ch'), may hold values from -6 to 6
- short_filter: bfloat16 [128, 512], P(None, 'ch'), may hold values from -0.5 to 0.5
- decay_rates: float32 [512, 16], P('ch'), may hold values from 0.0001953125 to 0.04
- residues: float32 [512, 16], P('ch'), may hold values from -1.5 to 1.5
Outputs:
- mixed: bfloat16 [1024, 8192], P('ctx', 'ch')
The draws below stay inside these ranges and needn't reach their ends.
All inputs are finite; a program needn't handle non-finite values.
Results may differ from the reference program's by a relative error of at most 0.0065.
Values may be sent and summed in bfloat16 or wider, within the bound.
A program may use at most 64 MiB of HBM per device.

```python
import math
import jax
import jax.numpy as jnp
from jax import lax

D = 8192
TAPS = 128
ORDER = 16
SEQ = 1024
GROUPS = 512


def block_levels(key, extent, split, low, largest):
    factor_of = 1.0
    for dim, shards_of in split:
        heights = jax.random.uniform(jax.random.fold_in(jax.random.fold_in(key, 6), dim), (shards_of,), jnp.float32, low / len(split), largest / len(split))
        factor_of = factor_of * jnp.repeat(jnp.exp(heights), extent[dim] // shards_of).reshape((-1,) + (1,) * (len(extent) - 1 - dim))
    return factor_of


def bell_draw(own_key, extent, deviation, bound, cuts=(), held_as=jnp.bfloat16):
    factor_of = block_levels(own_key, extent, cuts, -0.22, 0.18) if cuts else 1.0
    values = jax.random.normal(own_key, extent, jnp.float32) * deviation * factor_of
    return jnp.minimum(jnp.maximum(values, -bound), bound).astype(held_as)


def setup_inputs(seed: int = 0) -> dict:
    splits = jax.random.split(jax.random.key(seed), 9)
    q_short = bell_draw(splits[0], (SEQ, D), 1.0, 6.0, ((0, 8), (1, 4)))
    k_short = bell_draw(splits[1], (SEQ, D), 1.0, 6.0, ((0, 8), (1, 4)))
    v_input = bell_draw(splits[2], (SEQ, D), 1.0, 6.0, ((0, 8), (1, 4)))
    q_long = bell_draw(splits[3], (SEQ, D), 1.0, 6.0, ((0, 8), (1, 4)))
    k_long = bell_draw(splits[4], (SEQ, D), 1.0, 6.0, ((0, 8), (1, 4)))
    short_filter = bell_draw(splits[5], (TAPS, GROUPS), TAPS ** -0.5, 0.5, ((1, 4),))
    decay_rates = jnp.clip(jnp.exp(math.log(0.04) - 5.322034 * jax.random.uniform(splits[6], (GROUPS, ORDER), jnp.float32) ** block_levels(splits[6], (GROUPS, ORDER), ((0, 4),), -0.2, 0.2)), 0.0001953125, 0.04)
    residues = bell_draw(splits[7], (GROUPS, ORDER), ORDER ** -0.5, 1.5, ((0, 4),), jnp.float32)
    return dict(q_short=q_short, k_short=k_short, v_input=v_input, q_long=q_long, k_long=k_long, short_filter=short_filter, decay_rates=decay_rates, residues=residues)


def mode_filter(positions, rates, weights):
    scaled = weights * jnp.sqrt(2.0 * rates)
    return lax.optimization_barrier(jnp.sum(scaled[None] * jnp.exp(-rates[None] * positions[:, None, None]), axis=-1))

def lag_matrix(column):
    reversed_col = jnp.concatenate([column[:1], column[:0:-1]], 0)
    tiled = jnp.tile(reversed_col, (128, 1))[:128 * 255]
    return tiled.reshape(128, 255, column.shape[1])[:, :128]

def short_tables(short_taps):
    blank = jnp.zeros_like(short_taps)
    near_table = lag_matrix(jnp.concatenate([short_taps, blank], 0))
    far_table = lag_matrix(jnp.concatenate([blank, short_taps], 0))
    return (near_table, far_table)

def reference(q_short, k_short, v_input, q_long, k_long, short_filter, decay_rates, residues):
    channels = q_short.shape[1]
    block_size = min(256, channels)
    blocks_total = channels // block_size
    group_block = block_size // 16
    positions = jnp.arange(SEQ).astype(jnp.float32)
    near_table, far_table = short_tables(short_filter.astype(jnp.float32))

    def by_block(array):
        return array.reshape(array.shape[0], blocks_total, block_size).transpose(1, 0, 2)

    def table_block(table):
        return table.reshape(128, 128, blocks_total, group_block).transpose(2, 0, 1, 3)
    stacked = (by_block(q_short), by_block(k_short), by_block(v_input), by_block(q_long), by_block(k_long), table_block(near_table), table_block(far_table), decay_rates.reshape(blocks_total, group_block, ORDER), residues.reshape(blocks_total, group_block, ORDER))
    highest = lax.Precision.HIGHEST

    def mixing(pieces):
        query_short, key_short, value_in, query_long, key_long, near_piece, far_piece, rates_piece, weights_piece = pieces
        u_short = lax.optimization_barrier((key_short.astype(jnp.float32) * value_in.astype(jnp.float32)).astype(jnp.bfloat16)).astype(jnp.float32)
        padded = jnp.concatenate([jnp.zeros((128, block_size), jnp.float32), u_short], 0)
        padded = padded.reshape(SEQ // 128 + 1, 128, group_block, 16)
        y_short = jnp.einsum('tsg,bsgk->btgk', near_piece, padded[1:], precision=highest)
        y_short = y_short + jnp.einsum('tsg,bsgk->btgk', far_piece, padded[:-1], precision=highest)
        y_short = y_short.reshape(SEQ, block_size)
        u_long = key_long.astype(jnp.float32) * query_short.astype(jnp.float32) * y_short
        u_long = lax.optimization_barrier(u_long.astype(jnp.bfloat16)).astype(jnp.float32)
        length = 2 * SEQ
        filt = mode_filter(positions, rates_piece, weights_piece)
        spectrum = jnp.repeat(jnp.fft.rfft(filt, n=length, axis=0), 16, axis=1)
        y_long = jnp.fft.irfft(jnp.fft.rfft(u_long, n=length, axis=0) * spectrum, n=length, axis=0)[:SEQ]
        y_long = lax.optimization_barrier(y_long.astype(jnp.bfloat16)).astype(jnp.float32)
        return (query_long.astype(jnp.float32) * y_long).astype(jnp.bfloat16)
    mixed = lax.map(mixing, stacked)
    return mixed.transpose(1, 0, 2).reshape(SEQ, channels)
```

```python
import functools

import jax
import jax.numpy as jnp
from jax import lax
from jax.experimental import pallas as pl
from jax.experimental.pallas import tpu as pltpu
from jax.sharding import PartitionSpec as P

MESH = pl.DeviceIdType.MESH
LANES = 128
F32 = jnp.float32
BF16 = jnp.bfloat16


def iota(shape, dim):
    return lax.broadcasted_iota(jnp.int32, shape, dim)


def split(x):
    hi = x.astype(BF16)
    return hi, (x - hi.astype(F32)).astype(BF16)


def kernel(
    n, chunks, q_short, k_short, v_input, q_long, k_long, taps, rates, weights, out,
    ubuf, ulong, ynear, short_tab, long_tab, in_tab, out_tab, lam_rc, short_row, long_row, modes,
    state, psend, precv, halo_send, halo_recv, scan_send, scan_recv,
):
    me = lax.axis_index("ctx")
    tokens, ch = q_short.shape
    groups, order = rates.shape
    share = ch // groups
    per = LANES // share
    blocks = ch // LANES
    per_chunk = blocks // chunks
    width = per_chunk * LANES
    levels = n.bit_length() - 1

    barrier = pltpu.get_barrier_semaphore()
    for step in range(1, n):
        pl.semaphore_signal(
            barrier, inc=1, device_id={"ctx": lax.rem(me + step, n)}, device_id_type=MESH
        )

    ubuf[pl.ds(tokens, tokens), :] = (k_short[...].astype(F32) * v_input[...].astype(F32)).astype(BF16)

    pl.semaphore_wait(barrier, n - 1)

    def halo(c):
        cols = pl.ds(c * width, width)
        return pltpu.make_async_remote_copy(
            src_ref=ubuf.at[pl.ds(tokens, tokens), cols],
            dst_ref=ubuf.at[pl.ds(0, tokens), cols],
            send_sem=halo_send.at[c],
            recv_sem=halo_recv.at[c],
            device_id={"ctx": lax.rem(me + 1, n)},
            device_id_type=MESH,
        )

    @pl.when(me < n - 1)
    def _():
        for c in range(chunks):
            halo(c).start()

    @pl.when(me == 0)
    def _():
        ubuf[pl.ds(0, tokens), :] = jnp.zeros((tokens, ch), BF16)

    rate = rates[...]
    scaled = weights[...] * jnp.sqrt(2.0 * rate)
    reverse = lax.rem(tokens - iota((1, tokens), 1), tokens).astype(F32)
    total = jnp.zeros((groups, tokens), F32)
    for r in range(order):
        total = total + scaled[:, r : r + 1] * jnp.exp(-rate[:, r : r + 1] * reverse)
    long_row[...] = total
    flip = (lax.rem(iota((tokens, tokens), 0) + iota((tokens, tokens), 1), tokens) == 0).astype(BF16)
    taps_t = jnp.transpose(taps[...].astype(F32)).astype(BF16)
    short_row[...] = jnp.dot(taps_t, flip, preferred_element_type=F32)

    spread = (lax.rem(iota((order, LANES), 1), order) == iota((order, LANES), 0)).astype(F32)
    own = lax.rem(iota((groups, LANES), 0), per) == iota((groups, LANES), 1) // order

    def row_modes(x):
        wide = jnp.dot(x, spread, precision=lax.Precision.HIGHEST, preferred_element_type=F32)
        return jnp.where(own, wide, 0.0)

    rate_wide = row_modes(rate)
    modes[0] = jnp.sum(rate_wide.reshape(blocks, per, LANES), axis=1)
    modes[1] = jnp.sum(row_modes(scaled).reshape(blocks, per, LANES), axis=1)
    rate_tall = jnp.transpose(rate_wide)

    diag = iota((LANES, LANES), 0) // order == iota((LANES, LANES), 1) // share
    lower = iota((tokens, tokens), 0) >= iota((tokens, tokens), 1)

    def compact(x):
        return jnp.sum(jnp.where(diag, x, 0.0).reshape(per, order, LANES), axis=0)

    for b in range(blocks):
        in_block = iota((LANES, groups), 1) // per == b
        column = jnp.sum(jnp.where(in_block, rate_tall, 0.0), axis=1, keepdims=True)
        lam_rc[:, pl.ds(b * LANES, LANES)] = compact(jnp.broadcast_to(column, (LANES, LANES)))
        ahead = (tokens - iota((LANES, tokens), 1)).astype(F32)
        hi, lo = split(jnp.exp(-column * ahead))
        in_tab[b, :, pl.ds(0, tokens)] = hi
        in_tab[b, :, pl.ds(tokens, tokens)] = lo
        rows = iota((tokens, LANES), 0).astype(F32)
        hi, lo = split(modes[1, b : b + 1, :] * jnp.exp(-modes[0, b : b + 1, :] * rows))
        out_tab[b, :, pl.ds(0, LANES)] = hi
        out_tab[b, :, pl.ds(LANES, LANES)] = lo
        out_tab[b, :, pl.ds(2 * LANES, LANES)] = hi

    def tables(b, carry):
        at = pl.multiple_of(b * per, per)
        short8 = short_row[pl.ds(at, per), :]
        long8 = long_row[pl.ds(at, per), :]
        for g in range(per):
            turned = pltpu.roll(
                jnp.broadcast_to(short8[g : g + 1, :], (tokens, tokens)), 0, 1, stride=1, stride_axis=0
            )
            short_tab[b, pl.ds(g * tokens, tokens), pl.ds(0, tokens)] = jnp.where(lower, 0.0, turned).astype(BF16)
            short_tab[b, pl.ds(g * tokens, tokens), pl.ds(tokens, tokens)] = jnp.where(lower, turned, 0.0).astype(BF16)
            turned = pltpu.roll(
                jnp.broadcast_to(long8[g : g + 1, :], (tokens, tokens)), 0, 1, stride=1, stride_axis=0
            )
            long_tab[b, :, pl.ds(g * tokens, tokens)] = jnp.where(lower, turned, 0.0).astype(BF16)
        return carry

    lax.fori_loop(0, blocks, tables, 0)

    lane_group = iota((tokens, LANES), 1) // share

    def short_block(b, carry):
        cols = pl.ds(pl.multiple_of(b * LANES, LANES), LANES)
        full = jnp.dot(short_tab[b], ubuf[:, cols], preferred_element_type=F32)
        y = full[:tokens]
        for g in range(1, per):
            y = jnp.where(lane_group == g, full[g * tokens : (g + 1) * tokens], y)
        u = (k_long[:, cols].astype(F32) * q_short[:, cols].astype(F32) * y).astype(BF16)
        ulong[:, cols] = u
        local = jnp.dot(in_tab[b], jnp.concatenate([u, u], 0), preferred_element_type=F32)
        psend[0, :, cols] = compact(local)
        return carry

    def long_block(b, carry):
        cols = pl.ds(pl.multiple_of(b * LANES, LANES), LANES)
        u = ulong[:, cols]
        wide = jnp.concatenate(
            [jnp.where(lane_group == g, u, jnp.zeros_like(u)) for g in range(per)], 0
        )
        ynear[:, cols] = jnp.dot(long_tab[b], wide, preferred_element_type=F32)
        return carry

    def final_block(b, carry):
        cols = pl.ds(pl.multiple_of(b * LANES, LANES), LANES)
        tall = jnp.where(diag, jnp.concatenate([state[:, cols]] * per, 0), 0.0)
        hi, lo = split(tall)
        far = jnp.dot(out_tab[b], jnp.concatenate([hi, hi, lo], 0), preferred_element_type=F32)
        y = (ynear[:, cols] + far).astype(BF16)
        out[:, cols] = (q_long[:, cols].astype(F32) * y.astype(F32)).astype(BF16)
        return carry

    def scan_copy(k, c, away):
        cols = pl.ds(c * width, width)
        return pltpu.make_async_remote_copy(
            src_ref=psend.at[k, :, cols],
            dst_ref=precv.at[k, :, cols],
            send_sem=scan_send.at[k, c, away],
            recv_sem=scan_recv.at[k, c],
            device_id={"ctx": lax.rem(me + 1 + away, n)},
            device_id_type=MESH,
        )

    def sends(k):
        return lax.rem(me, 2 << k) == (1 << k) - 1

    def scan_send_level(k, c):
        @pl.when(sends(k))
        def _():
            for away in range(1 << k):
                scan_copy(k, c, away).start()

    def scan_take_level(k, c):
        cols = pl.ds(c * width, width)

        @pl.when(lax.rem(me, 2 << k) >= (1 << k))
        def _():
            scan_copy(k, c, 0).wait_recv()
            distance = lax.rem(me, 1 << k) * tokens
            decay = jnp.exp(-lam_rc[:, cols] * distance.astype(F32))
            state[:, cols] = state[:, cols] + decay * precv[k, :, cols]

        if k + 1 < levels:
            decay = jnp.exp(-lam_rc[:, cols] * float(tokens))
            psend[k + 1, :, cols] = psend[0, :, cols] + decay * state[:, cols]

    state[...] = jnp.zeros_like(state)
    for stage in range(chunks + levels):
        if stage < chunks:
            c = stage

            @pl.when(me > 0)
            def _():
                halo(c).wait_recv()

            lax.fori_loop(c * per_chunk, (c + 1) * per_chunk, short_block, 0)
            scan_send_level(0, c)
        for k in range(levels):
            c = stage - 1 - k
            if 0 <= c < chunks:
                scan_take_level(k, c)
                if k + 1 < levels:
                    scan_send_level(k + 1, c)
        c = stage - levels
        if 0 <= stage - 1 < chunks:
            c = stage - 1
            lax.fori_loop(c * per_chunk, (c + 1) * per_chunk, long_block, 0)
    lax.fori_loop(0, blocks, final_block, 0)

    @pl.when(me < n - 1)
    def _():
        for c in range(chunks):
            halo(c).wait_send()

    for k in range(levels):

        @pl.when(sends(k))
        def _():
            for c in range(chunks):
                for away in range(1 << k):
                    scan_copy(k, c, away).wait_send()


def on_device(n, *args):
    q_short, taps, rates = args[0], args[5], args[6]
    tokens, ch = q_short.shape
    groups, order = rates.shape
    blocks = ch // LANES
    per = LANES * groups // ch
    chunks = max(c for c in (1, 2, 4) if blocks % c == 0)
    levels = n.bit_length() - 1
    dma = pltpu.SemaphoreType.DMA
    return pl.pallas_call(
        functools.partial(kernel, n, chunks),
        out_shape=jax.ShapeDtypeStruct((tokens, ch), BF16),
        in_specs=[pl.BlockSpec(memory_space=pltpu.VMEM)] * 8,
        out_specs=pl.BlockSpec(memory_space=pltpu.VMEM),
        scratch_shapes=[
            pltpu.VMEM((2 * tokens, ch), BF16),
            pltpu.VMEM((tokens, ch), BF16),
            pltpu.VMEM((tokens, ch), F32),
            pltpu.VMEM((blocks, per * tokens, 2 * tokens), BF16),
            pltpu.VMEM((blocks, tokens, per * tokens), BF16),
            pltpu.VMEM((blocks, LANES, 2 * tokens), BF16),
            pltpu.VMEM((blocks, tokens, 3 * LANES), BF16),
            pltpu.VMEM((order, ch), F32),
            pltpu.VMEM((groups, tokens), F32),
            pltpu.VMEM((groups, tokens), F32),
            pltpu.VMEM((2, blocks, LANES), F32),
            pltpu.VMEM((order, ch), F32),
            pltpu.VMEM((levels, order, ch), F32),
            pltpu.VMEM((levels, order, ch), F32),
            dma((chunks,)),
            dma((chunks,)),
            dma((levels, chunks, max(1, n // 2))),
            dma((levels, chunks)),
        ],
        compiler_params=pltpu.CompilerParams(
            collective_id=0, has_side_effects=True, vmem_limit_bytes=60 * 2**20
        ),
    )(*args)


def solution(mesh):
    in_specs = (P("ctx", "ch"),) * 5 + (P(None, "ch"), P("ch", None), P("ch", None))
    return jax.shard_map(
        functools.partial(on_device, mesh.shape["ctx"]),
        mesh=mesh,
        in_specs=in_specs,
        out_specs=P("ctx", "ch"),
        check_vma=False,
    )
```

```python
import functools

import jax
import jax.numpy as jnp
from jax import lax
from jax.experimental import pallas as pl
from jax.experimental.pallas import tpu as pltpu
from jax.sharding import PartitionSpec as P

MESH = pl.DeviceIdType.MESH
LANES = 128
F32 = jnp.float32
BF16 = jnp.bfloat16


def iota(shape, dim):
    return lax.broadcasted_iota(jnp.int32, shape, dim)


def split(x):
    hi = x.astype(BF16)
    return hi, (x - hi.astype(F32)).astype(BF16)


def kernel(
    n, chunks, q_short_in, k_short, v_input, q_long_in, k_long_in, taps, rates, weights, out,
    q_short, q_long, k_long, fetch_sem,
    ubuf, ulong, ynear, short_tab, long_tab, in_tab, out_tab, lam_rc, short_row, long_row, modes,
    state, psend, precv, halo_send, halo_recv, scan_send, scan_recv,
):
    me = lax.axis_index("ctx")
    tokens, ch = k_short.shape
    half = tokens // 2
    order, groups = rates.shape
    share = ch // groups
    per = LANES // share
    blocks = ch // LANES
    per_chunk = blocks // chunks
    width = per_chunk * LANES
    levels = n.bit_length() - 1

    barrier = pltpu.get_barrier_semaphore()
    for step in range(1, n):
        pl.semaphore_signal(
            barrier, inc=1, device_id={"ctx": lax.rem(me + step, n)}, device_id_type=MESH
        )

    fetches = [
        pltpu.make_async_copy(source, target, fetch_sem.at[i])
        for i, (source, target) in enumerate(
            ((q_short_in, q_short), (k_long_in, k_long), (q_long_in, q_long))
        )
    ]
    for fetch in fetches:
        fetch.start()

    ubuf[pl.ds(tokens, tokens), :] = (k_short[...].astype(F32) * v_input[...].astype(F32)).astype(BF16)

    pl.semaphore_wait(barrier, n - 1)

    def halo(c):
        cols = pl.ds(c * width, width)
        return pltpu.make_async_remote_copy(
            src_ref=ubuf.at[pl.ds(tokens, tokens), cols],
            dst_ref=ubuf.at[pl.ds(0, tokens), cols],
            send_sem=halo_send.at[c],
            recv_sem=halo_recv.at[c],
            device_id={"ctx": lax.rem(me + 1, n)},
            device_id_type=MESH,
        )

    @pl.when(me < n - 1)
    def _():
        for c in range(chunks):
            halo(c).start()

    @pl.when(me == 0)
    def _():
        ubuf[pl.ds(0, tokens), :] = jnp.zeros((tokens, ch), BF16)

    ubuf[pl.ds(2 * tokens, half), :] = jnp.zeros((half, ch), BF16)
    ulong[pl.ds(0, half), :] = jnp.zeros((half, ch), BF16)

    rate = jnp.transpose(rates[...])
    scaled = jnp.transpose(weights[...]) * jnp.sqrt(2.0 * rate)
    reverse = lax.rem(tokens - iota((1, tokens), 1), tokens).astype(F32)
    total = jnp.zeros((groups, tokens), F32)
    for r in range(order):
        total = total + scaled[:, r : r + 1] * jnp.exp(-rate[:, r : r + 1] * reverse)
    long_row[...] = total
    flip = (lax.rem(iota((tokens, tokens), 0) + iota((tokens, tokens), 1), tokens) == 0).astype(BF16)
    taps_t = jnp.transpose(taps[...].astype(F32)).astype(BF16)
    short_row[...] = jnp.dot(taps_t, flip, preferred_element_type=F32)

    spread = (lax.rem(iota((order, LANES), 1), order) == iota((order, LANES), 0)).astype(F32)
    own = lax.rem(iota((groups, LANES), 0), per) == iota((groups, LANES), 1) // order

    def row_modes(x):
        wide = jnp.dot(x, spread, precision=lax.Precision.HIGHEST, preferred_element_type=F32)
        return jnp.where(own, wide, 0.0)

    rate_wide = row_modes(rate)
    modes[0] = jnp.sum(rate_wide.reshape(blocks, per, LANES), axis=1)
    modes[1] = jnp.sum(row_modes(scaled).reshape(blocks, per, LANES), axis=1)
    rate_tall = jnp.transpose(rate_wide)

    diag = iota((LANES, LANES), 0) // order == iota((LANES, LANES), 1) // share
    rows_half = iota((half, tokens), 0)
    lower = rows_half >= iota((half, tokens), 1)
    causal = rows_half + half >= iota((half, tokens), 1)

    def compact(x):
        return jnp.sum(jnp.where(diag, x, 0.0).reshape(per, order, LANES), axis=0)

    for b in range(blocks):
        in_block = iota((LANES, groups), 1) // per == b
        column = jnp.sum(jnp.where(in_block, rate_tall, 0.0), axis=1, keepdims=True)
        lam_rc[:, pl.ds(b * LANES, LANES)] = compact(jnp.broadcast_to(column, (LANES, LANES)))
        ahead = (tokens - iota((LANES, tokens), 1)).astype(F32)
        hi, lo = split(jnp.exp(-column * ahead))
        in_tab[b, :, pl.ds(0, tokens)] = hi
        in_tab[b, :, pl.ds(tokens, tokens)] = lo
        rows = iota((tokens, LANES), 0).astype(F32)
        hi, lo = split(modes[1, b : b + 1, :] * jnp.exp(-modes[0, b : b + 1, :] * rows))
        out_tab[b, :, pl.ds(0, LANES)] = hi
        out_tab[b, :, pl.ds(LANES, LANES)] = lo
        out_tab[b, :, pl.ds(2 * LANES, LANES)] = hi

    def tables(b, carry):
        at = pl.multiple_of(b * per, per)
        short8 = short_row[pl.ds(at, per), :]
        long8 = long_row[pl.ds(at, per), :]
        for g in range(per):
            turned = pltpu.roll(
                jnp.broadcast_to(short8[g : g + 1, :], (half, tokens)), 0, 1, stride=1, stride_axis=0
            )
            short_tab[b, pl.ds(g * half, half), pl.ds(0, tokens)] = jnp.where(lower, 0.0, turned).astype(BF16)
            short_tab[b, pl.ds(g * half, half), pl.ds(tokens, tokens)] = jnp.where(lower, turned, 0.0).astype(BF16)
            turned = pltpu.roll(
                jnp.broadcast_to(long8[g : g + 1, :], (half, tokens)), half, 1, stride=1, stride_axis=0
            )
            long_tab[b, :, pl.ds(g * tokens, tokens)] = jnp.where(causal, turned, 0.0).astype(BF16)
        return carry

    lax.fori_loop(0, blocks, tables, 0, unroll=2)
    fetches[0].wait()
    fetches[1].wait()

    lane_group = lax.rem(iota((half, 2 * LANES), 1), LANES) // share
    lane_group_tall = lax.rem(iota((tokens, 2 * LANES), 1), LANES) // share

    def windows(x):
        return jnp.concatenate([x[:, :LANES], x[:, LANES:]], 0)

    def short_block(b, carry):
        cols = pl.ds(pl.multiple_of(b * LANES, LANES), LANES)
        pair = jnp.concatenate([ubuf[pl.ds(0, 2 * tokens), cols], ubuf[pl.ds(half, 2 * tokens), cols]], 1)
        full = jnp.dot(short_tab[b], pair, preferred_element_type=F32)
        y = full[:half]
        for g in range(1, per):
            y = jnp.where(lane_group == g, full[g * half : (g + 1) * half], y)
        y = windows(y)
        u = (k_long[:, cols].astype(F32) * q_short[:, cols].astype(F32) * y).astype(BF16)
        ulong[pl.ds(half, tokens), cols] = u
        local = jnp.dot(in_tab[b], jnp.concatenate([u, u], 0), preferred_element_type=F32)
        psend[0, :, cols] = compact(local)
        return carry

    def long_block(b, carry):
        cols = pl.ds(pl.multiple_of(b * LANES, LANES), LANES)
        u = jnp.concatenate([ulong[pl.ds(0, tokens), cols], ulong[pl.ds(half, tokens), cols]], 1)
        wide = jnp.concatenate(
            [jnp.where(lane_group_tall == g, u, jnp.zeros_like(u)) for g in range(per)], 0
        )
        ynear[:, cols] = windows(jnp.dot(long_tab[b], wide, preferred_element_type=F32))
        return carry

    def final_block(b, carry):
        cols = pl.ds(pl.multiple_of(b * LANES, LANES), LANES)
        tall = jnp.where(diag, jnp.concatenate([state[:, cols]] * per, 0), 0.0)
        hi, lo = split(tall)
        far = jnp.dot(out_tab[b], jnp.concatenate([hi, hi, lo], 0), preferred_element_type=F32)
        y = (ynear[:, cols] + far).astype(BF16)
        out[:, cols] = (q_long[:, cols].astype(F32) * y.astype(F32)).astype(BF16)
        return carry

    def scan_copy(k, c, away):
        cols = pl.ds(c * width, width)
        return pltpu.make_async_remote_copy(
            src_ref=psend.at[k, :, cols],
            dst_ref=precv.at[k, :, cols],
            send_sem=scan_send.at[k, c, away],
            recv_sem=scan_recv.at[k, c],
            device_id={"ctx": lax.rem(me + 1 + away, n)},
            device_id_type=MESH,
        )

    def sends(k):
        return lax.rem(me, 2 << k) == (1 << k) - 1

    def scan_send_level(k, c):
        @pl.when(sends(k))
        def _():
            for away in range(1 << k):
                scan_copy(k, c, away).start()

    def scan_take_level(k, c):
        cols = pl.ds(c * width, width)

        @pl.when(lax.rem(me, 2 << k) >= (1 << k))
        def _():
            scan_copy(k, c, 0).wait_recv()
            distance = lax.rem(me, 1 << k) * tokens
            decay = jnp.exp(-lam_rc[:, cols] * distance.astype(F32))
            state[:, cols] = state[:, cols] + decay * precv[k, :, cols]

        if k + 1 < levels:
            decay = jnp.exp(-lam_rc[:, cols] * float(tokens))
            psend[k + 1, :, cols] = psend[0, :, cols] + decay * state[:, cols]

    state[...] = jnp.zeros_like(state)
    for stage in range(chunks + levels):
        if stage < chunks:
            c = stage

            @pl.when(me > 0)
            def _():
                halo(c).wait_recv()

            lax.fori_loop(c * per_chunk, (c + 1) * per_chunk, short_block, 0, unroll=True)
            scan_send_level(0, c)
        for k in range(levels):
            c = stage - 1 - k
            if 0 <= c < chunks:
                scan_take_level(k, c)
                if k + 1 < levels:
                    scan_send_level(k + 1, c)
        c = stage - levels
        if 0 <= stage - 1 < chunks:
            c = stage - 1
            lax.fori_loop(c * per_chunk, (c + 1) * per_chunk, long_block, 0, unroll=True)
    fetches[2].wait()
    lax.fori_loop(0, blocks, final_block, 0, unroll=4)

    @pl.when(me < n - 1)
    def _():
        for c in range(chunks):
            halo(c).wait_send()

    for k in range(levels):

        @pl.when(sends(k))
        def _():
            for c in range(chunks):
                for away in range(1 << k):
                    scan_copy(k, c, away).wait_send()


def on_device(n, *args):
    args = args[:6] + (args[6].T, args[7].T)
    q_short, taps, rates = args[0], args[5], args[6]
    tokens, ch = q_short.shape
    order, groups = rates.shape
    blocks = ch // LANES
    per = LANES * groups // ch
    chunks = max(c for c in (1, 2, 4) if blocks % c == 0)
    levels = n.bit_length() - 1
    dma = pltpu.SemaphoreType.DMA
    return pl.pallas_call(
        functools.partial(kernel, n, chunks),
        out_shape=jax.ShapeDtypeStruct((tokens, ch), BF16),
        in_specs=[pl.BlockSpec(memory_space=pl.ANY if i in (0, 3, 4) else pltpu.VMEM) for i in range(8)],
        out_specs=pl.BlockSpec(memory_space=pltpu.VMEM),
        scratch_shapes=[
            pltpu.VMEM((tokens, ch), BF16),
            pltpu.VMEM((tokens, ch), BF16),
            pltpu.VMEM((tokens, ch), BF16),
            dma((3,)),
            pltpu.VMEM((2 * tokens + tokens // 2, ch), BF16),
            pltpu.VMEM((tokens + tokens // 2, ch), BF16),
            pltpu.VMEM((tokens, ch), F32),
            pltpu.VMEM((blocks, per * tokens // 2, 2 * tokens), BF16),
            pltpu.VMEM((blocks, tokens // 2, per * tokens), BF16),
            pltpu.VMEM((blocks, LANES, 2 * tokens), BF16),
            pltpu.VMEM((blocks, tokens, 3 * LANES), BF16),
            pltpu.VMEM((order, ch), F32),
            pltpu.VMEM((groups, tokens), F32),
            pltpu.VMEM((groups, tokens), F32),
            pltpu.VMEM((2, blocks, LANES), F32),
            pltpu.VMEM((order, ch), F32),
            pltpu.VMEM((levels, order, ch), F32),
            pltpu.VMEM((levels, order, ch), F32),
            dma((chunks,)),
            dma((chunks,)),
            dma((levels, chunks, max(1, n // 2))),
            dma((levels, chunks)),
        ],
        compiler_params=pltpu.CompilerParams(
            collective_id=0, has_side_effects=True, vmem_limit_bytes=60 * 2**20
        ),
    )(*args)


def solution(mesh):
    in_specs = (P("ctx", "ch"),) * 5 + (P(None, "ch"), P("ch", None), P("ch", None))
    return jax.shard_map(
        functools.partial(on_device, mesh.shape["ctx"]),
        mesh=mesh,
        in_specs=in_specs,
        out_specs=P("ctx", "ch"),
        check_vma=False,
    )
```

```python
import functools

import jax
import jax.numpy as jnp
from jax import lax
from jax.experimental import pallas as pl
from jax.experimental.pallas import tpu as pltpu
from jax.sharding import PartitionSpec as P

MESH = pl.DeviceIdType.MESH
LANES = 128
F32 = jnp.float32
BF16 = jnp.bfloat16


def iota(shape, dim):
    return lax.broadcasted_iota(jnp.int32, shape, dim)


def split(x):
    hi = x.astype(BF16)
    return hi, (x - hi.astype(F32)).astype(BF16)


def kernel(
    n, chunks, q_short_in, k_short, v_input, q_long_in, k_long_in, taps, rates, weights, out,
    q_short, q_long, k_long, fetch_sem,
    ubuf, ulong, ynear, short_tab, long_tab, in_tab, out_tab, lam_rc, short_row, long_row, modes,
    state, psend, precv, halo_send, halo_recv, scan_send, scan_recv,
):
    me = lax.axis_index("ctx")
    tokens, ch = k_short.shape
    half = tokens // 2
    order, groups = rates.shape
    share = ch // groups
    per = LANES // share
    blocks = ch // LANES
    per_chunk = blocks // chunks
    width = per_chunk * LANES
    levels = n.bit_length() - 1

    barrier = pltpu.get_barrier_semaphore()
    for step in range(1, n):
        pl.semaphore_signal(
            barrier, inc=1, device_id={"ctx": lax.rem(me + step, n)}, device_id_type=MESH
        )

    fetches = [
        pltpu.make_async_copy(source, target, fetch_sem.at[i])
        for i, (source, target) in enumerate(
            ((q_short_in, q_short), (k_long_in, k_long), (q_long_in, q_long))
        )
    ]
    for fetch in fetches:
        fetch.start()

    ubuf[pl.ds(tokens, tokens), :] = (k_short[...].astype(F32) * v_input[...].astype(F32)).astype(BF16)

    pl.semaphore_wait(barrier, n - 1)

    def halo(c):
        cols = pl.ds(c * width, width)
        return pltpu.make_async_remote_copy(
            src_ref=ubuf.at[pl.ds(tokens, tokens), cols],
            dst_ref=ubuf.at[pl.ds(0, tokens), cols],
            send_sem=halo_send.at[c],
            recv_sem=halo_recv.at[c],
            device_id={"ctx": lax.rem(me + 1, n)},
            device_id_type=MESH,
        )

    @pl.when(me < n - 1)
    def _():
        for c in range(chunks):
            halo(c).start()

    @pl.when(me == 0)
    def _():
        ubuf[pl.ds(0, tokens), :] = jnp.zeros((tokens, ch), BF16)

    ubuf[pl.ds(2 * tokens, half), :] = jnp.zeros((half, ch), BF16)
    ulong[pl.ds(0, half), :] = jnp.zeros((half, ch), BF16)

    rate = jnp.transpose(rates[...])
    scaled = jnp.transpose(weights[...]) * jnp.sqrt(2.0 * rate)
    reverse = lax.rem(tokens - iota((1, tokens), 1), tokens).astype(F32)
    total = jnp.zeros((groups, tokens), F32)
    for r in range(order):
        total = total + scaled[:, r : r + 1] * jnp.exp(-rate[:, r : r + 1] * reverse)
    long_row[...] = total
    flip = (lax.rem(iota((tokens, tokens), 0) + iota((tokens, tokens), 1), tokens) == 0).astype(BF16)
    taps_t = jnp.transpose(taps[...].astype(F32)).astype(BF16)
    short_row[...] = jnp.dot(taps_t, flip, preferred_element_type=F32)

    spread = (lax.rem(iota((order, LANES), 1), order) == iota((order, LANES), 0)).astype(F32)
    own = lax.rem(iota((groups, LANES), 0), per) == iota((groups, LANES), 1) // order

    def row_modes(x):
        wide = jnp.dot(x, spread, precision=lax.Precision.HIGHEST, preferred_element_type=F32)
        return jnp.where(own, wide, 0.0)

    rate_wide = row_modes(rate)
    modes[0] = jnp.sum(rate_wide.reshape(blocks, per, LANES), axis=1)
    modes[1] = jnp.sum(row_modes(scaled).reshape(blocks, per, LANES), axis=1)
    rate_tall = jnp.transpose(rate_wide)

    diag = iota((LANES, LANES), 0) // order == iota((LANES, LANES), 1) // share
    rows_half = iota((half, tokens), 0)
    lower = rows_half >= iota((half, tokens), 1)
    causal = rows_half + half >= iota((half, tokens), 1)

    def compact(x):
        return jnp.sum(jnp.where(diag, x, 0.0).reshape(per, order, LANES), axis=0)

    for b in range(blocks):
        in_block = iota((LANES, groups), 1) // per == b
        column = jnp.sum(jnp.where(in_block, rate_tall, 0.0), axis=1, keepdims=True)
        lam_rc[:, pl.ds(b * LANES, LANES)] = compact(jnp.broadcast_to(column, (LANES, LANES)))
        ahead = (tokens - iota((LANES, tokens), 1)).astype(F32)
        hi, lo = split(jnp.exp(-column * ahead))
        in_tab[b, :, pl.ds(0, tokens)] = hi
        in_tab[b, :, pl.ds(tokens, tokens)] = lo
        rows = iota((tokens, LANES), 0).astype(F32)
        hi, lo = split(modes[1, b : b + 1, :] * jnp.exp(-modes[0, b : b + 1, :] * rows))
        out_tab[b, :, pl.ds(0, LANES)] = hi
        out_tab[b, :, pl.ds(LANES, LANES)] = lo
        out_tab[b, :, pl.ds(2 * LANES, LANES)] = hi

    def tables(b, carry):
        at = pl.multiple_of(b * per, per)
        short8 = short_row[pl.ds(at, per), :]
        long8 = long_row[pl.ds(at, per), :]
        for g in range(per):
            turned = pltpu.roll(
                jnp.broadcast_to(short8[g : g + 1, :], (half, tokens)), 0, 1, stride=1, stride_axis=0
            )
            short_tab[b, pl.ds(g * half, half), pl.ds(0, tokens)] = jnp.where(lower, 0.0, turned).astype(BF16)
            short_tab[b, pl.ds(g * half, half), pl.ds(tokens, tokens)] = jnp.where(lower, turned, 0.0).astype(BF16)
            turned = pltpu.roll(
                jnp.broadcast_to(long8[g : g + 1, :], (half, tokens)), half, 1, stride=1, stride_axis=0
            )
            long_tab[b, :, pl.ds(g * tokens, tokens)] = jnp.where(causal, turned, 0.0).astype(BF16)
        return carry

    lax.fori_loop(0, blocks, tables, 0, unroll=2)
    fetches[0].wait()
    fetches[1].wait()

    lane_group = lax.rem(iota((half, 2 * LANES), 1), LANES) // share
    lane_group_tall = lax.rem(iota((tokens, 2 * LANES), 1), LANES) // share

    def windows(x):
        return jnp.concatenate([x[:, :LANES], x[:, LANES:]], 0)

    def short_block(b, carry):
        cols = pl.ds(pl.multiple_of(b * LANES, LANES), LANES)
        pair = jnp.concatenate([ubuf[pl.ds(0, 2 * tokens), cols], ubuf[pl.ds(half, 2 * tokens), cols]], 1)
        full = jnp.dot(short_tab[b], pair, preferred_element_type=F32)
        y = full[:half]
        for g in range(1, per):
            y = jnp.where(lane_group == g, full[g * half : (g + 1) * half], y)
        y = windows(y)
        u = (k_long[:, cols].astype(F32) * q_short[:, cols].astype(F32) * y).astype(BF16)
        ulong[pl.ds(half, tokens), cols] = u
        local = jnp.dot(in_tab[b], jnp.concatenate([u, u], 0), preferred_element_type=F32)
        psend[0, :, cols] = compact(local)
        return carry

    def long_block(b, carry):
        cols = pl.ds(pl.multiple_of(b * LANES, LANES), LANES)
        u = jnp.concatenate([ulong[pl.ds(0, tokens), cols], ulong[pl.ds(half, tokens), cols]], 1)
        wide = jnp.concatenate(
            [jnp.where(lane_group_tall == g, u, jnp.zeros_like(u)) for g in range(per)], 0
        )
        ynear[:, cols] = windows(jnp.dot(long_tab[b], wide, preferred_element_type=F32))
        return carry

    def final_block(b, carry):
        cols = pl.ds(pl.multiple_of(b * LANES, LANES), LANES)
        tall = jnp.where(diag, jnp.concatenate([state[:, cols]] * per, 0), 0.0)
        hi, lo = split(tall)
        far = jnp.dot(out_tab[b], jnp.concatenate([hi, hi, lo], 0), preferred_element_type=F32)
        y = (ynear[:, cols] + far).astype(BF16)
        out[:, cols] = (q_long[:, cols].astype(F32) * y.astype(F32)).astype(BF16)
        return carry

    def scan_copy(k, c, away):
        cols = pl.ds(c * width, width)
        return pltpu.make_async_remote_copy(
            src_ref=psend.at[k, :, cols],
            dst_ref=precv.at[k, :, cols],
            send_sem=scan_send.at[k, c, away],
            recv_sem=scan_recv.at[k, c],
            device_id={"ctx": lax.rem(me + 1 + away, n)},
            device_id_type=MESH,
        )

    def sends(k):
        return lax.rem(me, 2 << k) == (1 << k) - 1

    def scan_send_level(k, c):
        @pl.when(sends(k))
        def _():
            for away in range(1 << k):
                scan_copy(k, c, away).start()

    def scan_take_level(k, c):
        cols = pl.ds(c * width, width)

        @pl.when(lax.rem(me, 2 << k) >= (1 << k))
        def _():
            scan_copy(k, c, 0).wait_recv()
            distance = lax.rem(me, 1 << k) * tokens
            decay = jnp.exp(-lam_rc[:, cols] * distance.astype(F32))
            state[:, cols] = state[:, cols] + decay * precv[k, :, cols]

        if k + 1 < levels:
            decay = jnp.exp(-lam_rc[:, cols] * float(tokens))
            psend[k + 1, :, cols] = psend[0, :, cols] + decay * state[:, cols]

    def over(c, body):
        lax.fori_loop(c * per_chunk, (c + 1) * per_chunk, body, 0, unroll=True)

    def takes(stage):
        for k in range(levels):
            c = stage - 1 - k
            if 0 <= c < chunks:
                scan_take_level(k, c)
                if k + 1 < levels:
                    scan_send_level(k + 1, c)

    state[...] = jnp.zeros_like(state)
    for c in range(chunks):

        @pl.when(me > 0)
        def _():
            halo(c).wait_recv()

        over(c, short_block)
        scan_send_level(0, c)
        takes(c)
    fetches[2].wait()
    nears, ends = 0, 0
    for step in range(levels):
        stage = chunks + step
        goal = -(-chunks * (step + 1) // levels)
        while nears < goal:
            over(nears, long_block)
            nears += 1
        while ends < min(nears, stage - levels):
            over(ends, final_block)
            ends += 1
        takes(stage)
    for c in range(nears, chunks):
        over(c, long_block)
    for c in range(ends, chunks):
        over(c, final_block)

    @pl.when(me < n - 1)
    def _():
        for c in range(chunks):
            halo(c).wait_send()

    for k in range(levels):

        @pl.when(sends(k))
        def _():
            for c in range(chunks):
                for away in range(1 << k):
                    scan_copy(k, c, away).wait_send()


def on_device(n, *args):
    args = args[:6] + (args[6].T, args[7].T)
    q_short, taps, rates = args[0], args[5], args[6]
    tokens, ch = q_short.shape
    order, groups = rates.shape
    blocks = ch // LANES
    per = LANES * groups // ch
    chunks = max(c for c in (1, 2, 4) if blocks % c == 0)
    levels = n.bit_length() - 1
    dma = pltpu.SemaphoreType.DMA
    return pl.pallas_call(
        functools.partial(kernel, n, chunks),
        out_shape=jax.ShapeDtypeStruct((tokens, ch), BF16),
        in_specs=[pl.BlockSpec(memory_space=pl.ANY if i in (0, 3, 4) else pltpu.VMEM) for i in range(8)],
        out_specs=pl.BlockSpec(memory_space=pltpu.VMEM),
        scratch_shapes=[
            pltpu.VMEM((tokens, ch), BF16),
            pltpu.VMEM((tokens, ch), BF16),
            pltpu.VMEM((tokens, ch), BF16),
            dma((3,)),
            pltpu.VMEM((2 * tokens + tokens // 2, ch), BF16),
            pltpu.VMEM((tokens + tokens // 2, ch), BF16),
            pltpu.VMEM((tokens, ch), F32),
            pltpu.VMEM((blocks, per * tokens // 2, 2 * tokens), BF16),
            pltpu.VMEM((blocks, tokens // 2, per * tokens), BF16),
            pltpu.VMEM((blocks, LANES, 2 * tokens), BF16),
            pltpu.VMEM((blocks, tokens, 3 * LANES), BF16),
            pltpu.VMEM((order, ch), F32),
            pltpu.VMEM((groups, tokens), F32),
            pltpu.VMEM((groups, tokens), F32),
            pltpu.VMEM((2, blocks, LANES), F32),
            pltpu.VMEM((order, ch), F32),
            pltpu.VMEM((levels, order, ch), F32),
            pltpu.VMEM((levels, order, ch), F32),
            dma((chunks,)),
            dma((chunks,)),
            dma((levels, chunks, max(1, n // 2))),
            dma((levels, chunks)),
        ],
        compiler_params=pltpu.CompilerParams(
            collective_id=0, has_side_effects=True, vmem_limit_bytes=60 * 2**20
        ),
    )(*args)


def solution(mesh):
    in_specs = (P("ctx", "ch"),) * 5 + (P(None, "ch"), P("ch", None), P("ch", None))
    return jax.shard_map(
        functools.partial(on_device, mesh.shape["ctx"]),
        mesh=mesh,
        in_specs=in_specs,
        out_specs=P("ctx", "ch"),
        check_vma=False,
    )
```

```python
import functools

import jax
import jax.numpy as jnp
from jax import lax
from jax.experimental import pallas as pl
from jax.experimental.pallas import tpu as pltpu
from jax.sharding import PartitionSpec as P

MESH = pl.DeviceIdType.MESH
LANES = 128
F32 = jnp.float32
BF16 = jnp.bfloat16


def iota(shape, dim):
    return lax.broadcasted_iota(jnp.int32, shape, dim)


def split(x):
    hi = x.astype(BF16)
    return hi, (x - hi.astype(F32)).astype(BF16)


def kernel(
    n, chunks, q_short_in, k_short_in, v_input_in, q_long_in, k_long_in, taps, rates, weights, out,
    q_short, q_long, k_long, k_short, v_input, fetch_sem,
    ubuf, ulong, ynear, short_tab, long_tab, in_tab, out_tab, lam_rc, short_row, long_row, modes,
    state, psend, precv, halo_send, halo_recv, scan_send, scan_recv,
):
    me = lax.axis_index("ctx")
    tokens, ch = k_short_in.shape
    half = tokens // 2
    order, groups = rates.shape
    share = ch // groups
    per = LANES // share
    blocks = ch // LANES
    per_chunk = blocks // chunks
    width = per_chunk * LANES
    levels = n.bit_length() - 1

    barrier = pltpu.get_barrier_semaphore()
    for step in range(1, n):
        pl.semaphore_signal(
            barrier, inc=1, device_id={"ctx": lax.rem(me + step, n)}, device_id_type=MESH
        )

    fetches = [
        pltpu.make_async_copy(source, target, fetch_sem.at[i])
        for i, (source, target) in enumerate(
            (
                (q_short_in, q_short),
                (k_long_in, k_long),
                (q_long_in, q_long),
                (k_short_in, k_short),
                (v_input_in, v_input),
            )
        )
    ]
    for i in (3, 4, 0, 1, 2):
        fetches[i].start()
    fetches[3].wait()
    fetches[4].wait()

    ubuf[pl.ds(tokens, tokens), :] = (k_short[...].astype(F32) * v_input[...].astype(F32)).astype(BF16)

    pl.semaphore_wait(barrier, n - 1)

    def halo(c):
        cols = pl.ds(c * width, width)
        return pltpu.make_async_remote_copy(
            src_ref=ubuf.at[pl.ds(tokens, tokens), cols],
            dst_ref=ubuf.at[pl.ds(0, tokens), cols],
            send_sem=halo_send.at[c],
            recv_sem=halo_recv.at[c],
            device_id={"ctx": lax.rem(me + 1, n)},
            device_id_type=MESH,
        )

    @pl.when(me < n - 1)
    def _():
        for c in range(chunks):
            halo(c).start()

    @pl.when(me == 0)
    def _():
        ubuf[pl.ds(0, tokens), :] = jnp.zeros((tokens, ch), BF16)

    ubuf[pl.ds(2 * tokens, half), :] = jnp.zeros((half, ch), BF16)
    ulong[pl.ds(0, half), :] = jnp.zeros((half, ch), BF16)

    rate = jnp.transpose(rates[...])
    scaled = jnp.transpose(weights[...]) * jnp.sqrt(2.0 * rate)
    reverse = lax.rem(tokens - iota((1, tokens), 1), tokens).astype(F32)
    total = jnp.zeros((groups, tokens), F32)
    for r in range(order):
        total = total + scaled[:, r : r + 1] * jnp.exp(-rate[:, r : r + 1] * reverse)
    long_row[...] = total
    flip = (lax.rem(iota((tokens, tokens), 0) + iota((tokens, tokens), 1), tokens) == 0).astype(BF16)
    taps_t = jnp.transpose(taps[...].astype(F32)).astype(BF16)
    short_row[...] = jnp.dot(taps_t, flip, preferred_element_type=F32)

    spread = (lax.rem(iota((order, LANES), 1), order) == iota((order, LANES), 0)).astype(F32)
    own = lax.rem(iota((groups, LANES), 0), per) == iota((groups, LANES), 1) // order

    def row_modes(x):
        wide = jnp.dot(x, spread, precision=lax.Precision.HIGHEST, preferred_element_type=F32)
        return jnp.where(own, wide, 0.0)

    rate_wide = row_modes(rate)
    modes[0] = jnp.sum(rate_wide.reshape(blocks, per, LANES), axis=1)
    modes[1] = jnp.sum(row_modes(scaled).reshape(blocks, per, LANES), axis=1)
    rate_tall = jnp.transpose(rate_wide)

    diag = iota((LANES, LANES), 0) // order == iota((LANES, LANES), 1) // share
    rows_half = iota((half, tokens), 0)
    lower = rows_half >= iota((half, tokens), 1)
    causal = rows_half + half >= iota((half, tokens), 1)

    def compact(x):
        return jnp.sum(jnp.where(diag, x, 0.0).reshape(per, order, LANES), axis=0)

    for b in range(blocks):
        in_block = iota((LANES, groups), 1) // per == b
        column = jnp.sum(jnp.where(in_block, rate_tall, 0.0), axis=1, keepdims=True)
        lam_rc[:, pl.ds(b * LANES, LANES)] = compact(jnp.broadcast_to(column, (LANES, LANES)))
        ahead = (tokens - iota((LANES, tokens), 1)).astype(F32)
        hi, lo = split(jnp.exp(-column * ahead))
        in_tab[b, :, pl.ds(0, tokens)] = hi
        in_tab[b, :, pl.ds(tokens, tokens)] = lo
        rows = iota((tokens, LANES), 0).astype(F32)
        hi, lo = split(modes[1, b : b + 1, :] * jnp.exp(-modes[0, b : b + 1, :] * rows))
        out_tab[b, :, pl.ds(0, LANES)] = hi
        out_tab[b, :, pl.ds(LANES, LANES)] = lo
        out_tab[b, :, pl.ds(2 * LANES, LANES)] = hi

    def tables(b, carry):
        at = pl.multiple_of(b * per, per)
        short8 = short_row[pl.ds(at, per), :]
        long8 = long_row[pl.ds(at, per), :]
        for g in range(per):
            turned = pltpu.roll(
                jnp.broadcast_to(short8[g : g + 1, :], (half, tokens)), 0, 1, stride=1, stride_axis=0
            )
            short_tab[b, pl.ds(g * half, half), pl.ds(0, tokens)] = jnp.where(lower, 0.0, turned).astype(BF16)
            short_tab[b, pl.ds(g * half, half), pl.ds(tokens, tokens)] = jnp.where(lower, turned, 0.0).astype(BF16)
            turned = pltpu.roll(
                jnp.broadcast_to(long8[g : g + 1, :], (half, tokens)), half, 1, stride=1, stride_axis=0
            )
            long_tab[b, :, pl.ds(g * tokens, tokens)] = jnp.where(causal, turned, 0.0).astype(BF16)
        return carry

    lax.fori_loop(0, blocks, tables, 0, unroll=2)
    fetches[0].wait()
    fetches[1].wait()

    lane_group = lax.rem(iota((half, 2 * LANES), 1), LANES) // share
    lane_group_tall = lax.rem(iota((tokens, 2 * LANES), 1), LANES) // share

    def windows(x):
        return jnp.concatenate([x[:, :LANES], x[:, LANES:]], 0)

    def short_block(b, carry):
        cols = pl.ds(pl.multiple_of(b * LANES, LANES), LANES)
        pair = jnp.concatenate([ubuf[pl.ds(0, 2 * tokens), cols], ubuf[pl.ds(half, 2 * tokens), cols]], 1)
        full = jnp.dot(short_tab[b], pair, preferred_element_type=F32)
        y = full[:half]
        for g in range(1, per):
            y = jnp.where(lane_group == g, full[g * half : (g + 1) * half], y)
        y = windows(y)
        u = (k_long[:, cols].astype(F32) * q_short[:, cols].astype(F32) * y).astype(BF16)
        ulong[pl.ds(half, tokens), cols] = u
        local = jnp.dot(in_tab[b], jnp.concatenate([u, u], 0), preferred_element_type=F32)
        psend[0, :, cols] = compact(local)
        return carry

    def long_block(b, carry):
        cols = pl.ds(pl.multiple_of(b * LANES, LANES), LANES)
        u = jnp.concatenate([ulong[pl.ds(0, tokens), cols], ulong[pl.ds(half, tokens), cols]], 1)
        wide = jnp.concatenate(
            [jnp.where(lane_group_tall == g, u, jnp.zeros_like(u)) for g in range(per)], 0
        )
        ynear[:, cols] = windows(jnp.dot(long_tab[b], wide, preferred_element_type=F32))
        return carry

    def final_block(b, carry):
        cols = pl.ds(pl.multiple_of(b * LANES, LANES), LANES)
        tall = jnp.where(diag, jnp.concatenate([state[:, cols]] * per, 0), 0.0)
        hi, lo = split(tall)
        far = jnp.dot(out_tab[b], jnp.concatenate([hi, hi, lo], 0), preferred_element_type=F32)
        y = (ynear[:, cols] + far).astype(BF16)
        out[:, cols] = (q_long[:, cols].astype(F32) * y.astype(F32)).astype(BF16)
        return carry

    def scan_copy(k, c, away):
        cols = pl.ds(c * width, width)
        return pltpu.make_async_remote_copy(
            src_ref=psend.at[k, :, cols],
            dst_ref=precv.at[k, :, cols],
            send_sem=scan_send.at[k, c, away],
            recv_sem=scan_recv.at[k, c],
            device_id={"ctx": lax.rem(me + 1 + away, n)},
            device_id_type=MESH,
        )

    def sends(k):
        return lax.rem(me, 2 << k) == (1 << k) - 1

    def scan_send_level(k, c):
        @pl.when(sends(k))
        def _():
            for away in range(1 << k):
                scan_copy(k, c, away).start()

    def scan_take_level(k, c):
        cols = pl.ds(c * width, width)

        @pl.when(lax.rem(me, 2 << k) >= (1 << k))
        def _():
            scan_copy(k, c, 0).wait_recv()
            distance = lax.rem(me, 1 << k) * tokens
            decay = jnp.exp(-lam_rc[:, cols] * distance.astype(F32))
            state[:, cols] = state[:, cols] + decay * precv[k, :, cols]

        if k + 1 < levels:
            decay = jnp.exp(-lam_rc[:, cols] * float(tokens))
            psend[k + 1, :, cols] = psend[0, :, cols] + decay * state[:, cols]

    def over(c, body):
        lax.fori_loop(c * per_chunk, (c + 1) * per_chunk, body, 0, unroll=True)

    def takes(stage):
        for k in range(levels):
            c = stage - 1 - k
            if 0 <= c < chunks:
                scan_take_level(k, c)
                if k + 1 < levels:
                    scan_send_level(k + 1, c)

    state[...] = jnp.zeros_like(state)
    for c in range(chunks):

        @pl.when(me > 0)
        def _():
            halo(c).wait_recv()

        over(c, short_block)
        scan_send_level(0, c)
        takes(c)
    fetches[2].wait()
    nears, ends = 0, 0
    for step in range(levels):
        stage = chunks + step
        goal = -(-chunks * (step + 1) // levels)
        while nears < goal:
            over(nears, long_block)
            nears += 1
        while ends < min(nears, stage - levels):
            over(ends, final_block)
            ends += 1
        takes(stage)
    for c in range(nears, chunks):
        over(c, long_block)
    for c in range(ends, chunks):
        over(c, final_block)

    @pl.when(me < n - 1)
    def _():
        for c in range(chunks):
            halo(c).wait_send()

    for k in range(levels):

        @pl.when(sends(k))
        def _():
            for c in range(chunks):
                for away in range(1 << k):
                    scan_copy(k, c, away).wait_send()


def on_device(n, *args):
    args = args[:6] + (args[6].T, args[7].T)
    q_short, taps, rates = args[0], args[5], args[6]
    tokens, ch = q_short.shape
    order, groups = rates.shape
    blocks = ch // LANES
    per = LANES * groups // ch
    chunks = max(c for c in (1, 2, 4) if blocks % c == 0)
    levels = n.bit_length() - 1
    dma = pltpu.SemaphoreType.DMA
    return pl.pallas_call(
        functools.partial(kernel, n, chunks),
        out_shape=jax.ShapeDtypeStruct((tokens, ch), BF16),
        in_specs=[pl.BlockSpec(memory_space=pl.ANY if i < 5 else pltpu.VMEM) for i in range(8)],
        out_specs=pl.BlockSpec(memory_space=pltpu.VMEM),
        scratch_shapes=[
            pltpu.VMEM((tokens, ch), BF16),
            pltpu.VMEM((tokens, ch), BF16),
            pltpu.VMEM((tokens, ch), BF16),
            pltpu.VMEM((tokens, ch), BF16),
            pltpu.VMEM((tokens, ch), BF16),
            dma((5,)),
            pltpu.VMEM((2 * tokens + tokens // 2, ch), BF16),
            pltpu.VMEM((tokens + tokens // 2, ch), BF16),
            pltpu.VMEM((tokens, ch), F32),
            pltpu.VMEM((blocks, per * tokens // 2, 2 * tokens), BF16),
            pltpu.VMEM((blocks, tokens // 2, per * tokens), BF16),
            pltpu.VMEM((blocks, LANES, 2 * tokens), BF16),
            pltpu.VMEM((blocks, tokens, 3 * LANES), BF16),
            pltpu.VMEM((order, ch), F32),
            pltpu.VMEM((groups, tokens), F32),
            pltpu.VMEM((groups, tokens), F32),
            pltpu.VMEM((2, blocks, LANES), F32),
            pltpu.VMEM((order, ch), F32),
            pltpu.VMEM((levels, order, ch), F32),
            pltpu.VMEM((levels, order, ch), F32),
            dma((chunks,)),
            dma((chunks,)),
            dma((levels, chunks, max(1, n // 2))),
            dma((levels, chunks)),
        ],
        compiler_params=pltpu.CompilerParams(
            collective_id=0, has_side_effects=True, vmem_limit_bytes=60 * 2**20
        ),
    )(*args)


def solution(mesh):
    in_specs = (P("ctx", "ch"),) * 5 + (P(None, "ch"), P("ch", None), P("ch", None))
    return jax.shard_map(
        functools.partial(on_device, mesh.shape["ctx"]),
        mesh=mesh,
        in_specs=in_specs,
        out_specs=P("ctx", "ch"),
        check_vma=False,
    )
```

```python
import functools

import jax
import jax.numpy as jnp
from jax import lax
from jax.experimental import pallas as pl
from jax.experimental.pallas import tpu as pltpu
from jax.sharding import PartitionSpec as P

MESH = pl.DeviceIdType.MESH
LANES = 128
F32 = jnp.float32
BF16 = jnp.bfloat16


def iota(shape, dim):
    return lax.broadcasted_iota(jnp.int32, shape, dim)


def split(x):
    hi = x.astype(BF16)
    return hi, (x - hi.astype(F32)).astype(BF16)


def kernel(
    n, chunks, q_short_in, k_short_in, v_input_in, q_long_in, k_long_in, taps, rates, weights, out,
    q_short, q_long, k_long, k_short, v_input, fetch_sem,
    ubuf, ulong, ynear, short_tab, long_tab, in_tab, out_tab, lam_rc, short_row, long_row, modes,
    state, psend, precv, halo_send, halo_recv, scan_send, scan_recv,
):
    me = lax.axis_index("ctx")
    tokens, ch = k_short_in.shape
    half = tokens // 2
    order, groups = rates.shape
    share = ch // groups
    per = LANES // share
    blocks = ch // LANES
    per_chunk = blocks // chunks
    width = per_chunk * LANES
    levels = n.bit_length() - 1

    barrier = pltpu.get_barrier_semaphore()
    for step in range(1, n):
        pl.semaphore_signal(
            barrier, inc=1, device_id={"ctx": lax.rem(me + step, n)}, device_id_type=MESH
        )

    fetches = [
        pltpu.make_async_copy(source, target, fetch_sem.at[i])
        for i, (source, target) in enumerate(
            (
                (q_short_in, q_short),
                (k_long_in, k_long),
                (q_long_in, q_long),
                (k_short_in, k_short),
                (v_input_in, v_input),
            )
        )
    ]
    for i in (3, 4):
        fetches[i].start()
    fetches[3].wait()
    fetches[4].wait()
    for i in (0, 1, 2):
        fetches[i].start()

    ubuf[pl.ds(tokens, tokens), :] = (k_short[...].astype(F32) * v_input[...].astype(F32)).astype(BF16)

    pl.semaphore_wait(barrier, n - 1)

    def halo(c):
        cols = pl.ds(c * width, width)
        return pltpu.make_async_remote_copy(
            src_ref=ubuf.at[pl.ds(tokens, tokens), cols],
            dst_ref=ubuf.at[pl.ds(0, tokens), cols],
            send_sem=halo_send.at[c],
            recv_sem=halo_recv.at[c],
            device_id={"ctx": lax.rem(me + 1, n)},
            device_id_type=MESH,
        )

    @pl.when(me < n - 1)
    def _():
        for c in range(chunks):
            halo(c).start()

    @pl.when(me == 0)
    def _():
        ubuf[pl.ds(0, tokens), :] = jnp.zeros((tokens, ch), BF16)

    ubuf[pl.ds(2 * tokens, half), :] = jnp.zeros((half, ch), BF16)
    ulong[pl.ds(0, half), :] = jnp.zeros((half, ch), BF16)

    rate = jnp.transpose(rates[...])
    scaled = jnp.transpose(weights[...]) * jnp.sqrt(2.0 * rate)
    reverse = lax.rem(tokens - iota((1, tokens), 1), tokens).astype(F32)
    total = jnp.zeros((groups, tokens), F32)
    for r in range(order):
        total = total + scaled[:, r : r + 1] * jnp.exp(-rate[:, r : r + 1] * reverse)
    long_row[...] = total
    flip = (lax.rem(iota((tokens, tokens), 0) + iota((tokens, tokens), 1), tokens) == 0).astype(BF16)
    taps_t = jnp.transpose(taps[...].astype(F32)).astype(BF16)
    short_row[...] = jnp.dot(taps_t, flip, preferred_element_type=F32)

    spread = (lax.rem(iota((order, LANES), 1), order) == iota((order, LANES), 0)).astype(F32)
    own = lax.rem(iota((groups, LANES), 0), per) == iota((groups, LANES), 1) // order

    def row_modes(x):
        wide = jnp.dot(x, spread, precision=lax.Precision.HIGHEST, preferred_element_type=F32)
        return jnp.where(own, wide, 0.0)

    rate_wide = row_modes(rate)
    modes[0] = jnp.sum(rate_wide.reshape(blocks, per, LANES), axis=1)
    modes[1] = jnp.sum(row_modes(scaled).reshape(blocks, per, LANES), axis=1)
    rate_tall = jnp.transpose(rate_wide)

    diag = iota((LANES, LANES), 0) // order == iota((LANES, LANES), 1) // share
    rows_half = iota((half, tokens), 0)
    lower = rows_half >= iota((half, tokens), 1)
    causal = rows_half + half >= iota((half, tokens), 1)

    def compact(x):
        return jnp.sum(jnp.where(diag, x, 0.0).reshape(per, order, LANES), axis=0)

    for b in range(blocks):
        in_block = iota((LANES, groups), 1) // per == b
        column = jnp.sum(jnp.where(in_block, rate_tall, 0.0), axis=1, keepdims=True)
        lam_rc[:, pl.ds(b * LANES, LANES)] = compact(jnp.broadcast_to(column, (LANES, LANES)))
        ahead = (tokens - iota((LANES, tokens), 1)).astype(F32)
        hi, lo = split(jnp.exp(-column * ahead))
        in_tab[b, :, pl.ds(0, tokens)] = hi
        in_tab[b, :, pl.ds(tokens, tokens)] = lo
        rows = iota((tokens, LANES), 0).astype(F32)
        hi, lo = split(modes[1, b : b + 1, :] * jnp.exp(-modes[0, b : b + 1, :] * rows))
        out_tab[b, :, pl.ds(0, LANES)] = hi
        out_tab[b, :, pl.ds(LANES, LANES)] = lo
        out_tab[b, :, pl.ds(2 * LANES, LANES)] = hi

    def tables(b, carry):
        at = pl.multiple_of(b * per, per)
        short8 = short_row[pl.ds(at, per), :]
        long8 = long_row[pl.ds(at, per), :]
        for g in range(per):
            turned = pltpu.roll(
                jnp.broadcast_to(short8[g : g + 1, :], (half, tokens)), 0, 1, stride=1, stride_axis=0
            )
            short_tab[b, pl.ds(g * half, half), pl.ds(0, tokens)] = jnp.where(lower, 0.0, turned).astype(BF16)
            short_tab[b, pl.ds(g * half, half), pl.ds(tokens, tokens)] = jnp.where(lower, turned, 0.0).astype(BF16)
            turned = pltpu.roll(
                jnp.broadcast_to(long8[g : g + 1, :], (half, tokens)), half, 1, stride=1, stride_axis=0
            )
            long_tab[b, :, pl.ds(g * tokens, tokens)] = jnp.where(causal, turned, 0.0).astype(BF16)
        return carry

    lax.fori_loop(0, blocks, tables, 0, unroll=2)
    fetches[0].wait()
    fetches[1].wait()

    lane_group = lax.rem(iota((half, 2 * LANES), 1), LANES) // share
    lane_group_tall = lax.rem(iota((tokens, 2 * LANES), 1), LANES) // share

    def windows(x):
        return jnp.concatenate([x[:, :LANES], x[:, LANES:]], 0)

    def short_block(b, carry):
        cols = pl.ds(pl.multiple_of(b * LANES, LANES), LANES)
        pair = jnp.concatenate([ubuf[pl.ds(0, 2 * tokens), cols], ubuf[pl.ds(half, 2 * tokens), cols]], 1)
        full = jnp.dot(short_tab[b], pair, preferred_element_type=F32)
        y = full[:half]
        for g in range(1, per):
            y = jnp.where(lane_group == g, full[g * half : (g + 1) * half], y)
        y = windows(y)
        u = (k_long[:, cols].astype(F32) * q_short[:, cols].astype(F32) * y).astype(BF16)
        ulong[pl.ds(half, tokens), cols] = u
        local = jnp.dot(in_tab[b], jnp.concatenate([u, u], 0), preferred_element_type=F32)
        psend[0, :, cols] = compact(local)
        return carry

    def long_block(b, carry):
        cols = pl.ds(pl.multiple_of(b * LANES, LANES), LANES)
        u = jnp.concatenate([ulong[pl.ds(0, tokens), cols], ulong[pl.ds(half, tokens), cols]], 1)
        wide = jnp.concatenate(
            [jnp.where(lane_group_tall == g, u, jnp.zeros_like(u)) for g in range(per)], 0
        )
        ynear[:, cols] = windows(jnp.dot(long_tab[b], wide, preferred_element_type=F32))
        return carry

    def final_block(b, carry):
        cols = pl.ds(pl.multiple_of(b * LANES, LANES), LANES)
        tall = jnp.where(diag, jnp.concatenate([state[:, cols]] * per, 0), 0.0)
        hi, lo = split(tall)
        far = jnp.dot(out_tab[b], jnp.concatenate([hi, hi, lo], 0), preferred_element_type=F32)
        y = (ynear[:, cols] + far).astype(BF16)
        out[:, cols] = (q_long[:, cols].astype(F32) * y.astype(F32)).astype(BF16)
        return carry

    def scan_copy(k, c, away):
        cols = pl.ds(c * width, width)
        return pltpu.make_async_remote_copy(
            src_ref=psend.at[k, :, cols],
            dst_ref=precv.at[k, :, cols],
            send_sem=scan_send.at[k, c, away],
            recv_sem=scan_recv.at[k, c],
            device_id={"ctx": lax.rem(me + 1 + away, n)},
            device_id_type=MESH,
        )

    def sends(k):
        return lax.rem(me, 2 << k) == (1 << k) - 1

    def scan_send_level(k, c):
        @pl.when(sends(k))
        def _():
            for away in range(1 << k):
                scan_copy(k, c, away).start()

    def scan_take_level(k, c):
        cols = pl.ds(c * width, width)

        @pl.when(lax.rem(me, 2 << k) >= (1 << k))
        def _():
            scan_copy(k, c, 0).wait_recv()
            distance = lax.rem(me, 1 << k) * tokens
            decay = jnp.exp(-lam_rc[:, cols] * distance.astype(F32))
            state[:, cols] = state[:, cols] + decay * precv[k, :, cols]

        if k + 1 < levels:
            decay = jnp.exp(-lam_rc[:, cols] * float(tokens))
            psend[k + 1, :, cols] = psend[0, :, cols] + decay * state[:, cols]

    def over(c, body):
        lax.fori_loop(c * per_chunk, (c + 1) * per_chunk, body, 0, unroll=True)

    def takes(stage):
        for k in range(levels):
            c = stage - 1 - k
            if 0 <= c < chunks:
                scan_take_level(k, c)
                if k + 1 < levels:
                    scan_send_level(k + 1, c)

    state[...] = jnp.zeros_like(state)
    for c in range(chunks):

        @pl.when(me > 0)
        def _():
            halo(c).wait_recv()

        over(c, short_block)
        scan_send_level(0, c)
        takes(c)
    fetches[2].wait()
    nears, ends = 0, 0
    for step in range(levels):
        stage = chunks + step
        goal = -(-chunks * (step + 1) // levels)
        while nears < goal:
            over(nears, long_block)
            nears += 1
        while ends < min(nears, stage - levels):
            over(ends, final_block)
            ends += 1
        takes(stage)
    for c in range(nears, chunks):
        over(c, long_block)
    for c in range(ends, chunks):
        over(c, final_block)

    @pl.when(me < n - 1)
    def _():
        for c in range(chunks):
            halo(c).wait_send()

    for k in range(levels):

        @pl.when(sends(k))
        def _():
            for c in range(chunks):
                for away in range(1 << k):
                    scan_copy(k, c, away).wait_send()


def on_device(n, *args):
    args = args[:6] + (args[6].T, args[7].T)
    q_short, taps, rates = args[0], args[5], args[6]
    tokens, ch = q_short.shape
    order, groups = rates.shape
    blocks = ch // LANES
    per = LANES * groups // ch
    chunks = max(c for c in (1, 2, 4) if blocks % c == 0)
    levels = n.bit_length() - 1
    dma = pltpu.SemaphoreType.DMA
    return pl.pallas_call(
        functools.partial(kernel, n, chunks),
        out_shape=jax.ShapeDtypeStruct((tokens, ch), BF16),
        in_specs=[pl.BlockSpec(memory_space=pl.ANY if i < 5 else pltpu.VMEM) for i in range(8)],
        out_specs=pl.BlockSpec(memory_space=pltpu.VMEM),
        scratch_shapes=[
            pltpu.VMEM((tokens, ch), BF16),
            pltpu.VMEM((tokens, ch), BF16),
            pltpu.VMEM((tokens, ch), BF16),
            pltpu.VMEM((tokens, ch), BF16),
            pltpu.VMEM((tokens, ch), BF16),
            dma((5,)),
            pltpu.VMEM((2 * tokens + tokens // 2, ch), BF16),
            pltpu.VMEM((tokens + tokens // 2, ch), BF16),
            pltpu.VMEM((tokens, ch), F32),
            pltpu.VMEM((blocks, per * tokens // 2, 2 * tokens), BF16),
            pltpu.VMEM((blocks, tokens // 2, per * tokens), BF16),
            pltpu.VMEM((blocks, LANES, 2 * tokens), BF16),
            pltpu.VMEM((blocks, tokens, 3 * LANES), BF16),
            pltpu.VMEM((order, ch), F32),
            pltpu.VMEM((groups, tokens), F32),
            pltpu.VMEM((groups, tokens), F32),
            pltpu.VMEM((2, blocks, LANES), F32),
            pltpu.VMEM((order, ch), F32),
            pltpu.VMEM((levels, order, ch), F32),
            pltpu.VMEM((levels, order, ch), F32),
            dma((chunks,)),
            dma((chunks,)),
            dma((levels, chunks, max(1, n // 2))),
            dma((levels, chunks)),
        ],
        compiler_params=pltpu.CompilerParams(
            collective_id=0, has_side_effects=True, vmem_limit_bytes=60 * 2**20
        ),
    )(*args)


def solution(mesh):
    in_specs = (P("ctx", "ch"),) * 5 + (P(None, "ch"), P("ch", None), P("ch", None))
    return jax.shard_map(
        functools.partial(on_device, mesh.shape["ctx"]),
        mesh=mesh,
        in_specs=in_specs,
        out_specs=P("ctx", "ch"),
        check_vma=False,
    )
```
